768 devices in a mesh: dp: 48 (over z_hi, y, core), expert: 16 (over z_lo, x).
Axes of the slice: x: 4, y: 8, z: 12 (z_hi: 3, z_lo: 4; z = z_hi * 4 + z_lo), core: 2. Of those that a mesh axis runs over, the one named last changes fastest.
Arguments:
- tokens: bfloat16 [98304, 2048], P(('dp', 'expert')), may hold values from -6 to 6
- routes: int32 [98304, 1], P(('dp', 'expert')), may hold values from 0 to 15; in each aligned block of 128 rows (0 to 127, 128 to 255, ...) at most 10 rows name the same one
- route_gates: float32 [98304, 1], P(('dp', 'expert')), may hold values from 0.1 to 1
- w_gate: bfloat16 [16, 2048, 384], P('expert'), may hold values from -0.125 to 0.125
- w_up: bfloat16 [16, 2048, 384], P('expert'), may hold values from -0.125 to 0.125
- w_down: bfloat16 [16, 384, 2048], P('expert'), may hold values from -0.3125 to 0.3125
- cotangent: bfloat16 [98304, 2048], P(('dp', 'expert')), may hold values from -6 to 6
Outputs:
- mixed: bfloat16 [98304, 2048], P(('dp', 'expert'))
- d_tokens: bfloat16 [98304, 2048], P(('dp', 'expert'))
- d_gates: float32 [98304, 1], P(('dp', 'expert'))
- d_w_down: bfloat16 [16, 384, 2048], P('expert', 'dp')
The draws below stay inside these ranges and needn't reach their ends.
Inputs may be any that keep to these rules, and one draw needn't show every extreme that they name: `routes`: each token names exactly one expert. Among the rows of one device no expert is named more than 10 times, a bound that some block reaches in some devices' rows; every expert is named somewhere.
All inputs are finite; a program needn't handle non-finite values.
Results may differ from the reference program's by a relative error of at most 0.0058.
Values may be sent and summed in bfloat16 or wider, within the bound.
No kernel may reach another device: no remote copies, remote signals or barrier semaphores. Data moves between devices by JAX's collectives and lax.ppermute only.
A program may use at most 32 MiB of HBM per device.

```python
import math
import jax
import jax.numpy as jnp
import numpy as np
from jax import lax

D = 2048
FF = 384
TOK_DEV = 128
TOP = 1
EXPERTS = 16
CAP = 10
TOKENS = 98304
N_DP = 48
N_EXPERT = 16


def level_of(stream_key, extent, split, least, high):
    factor_of, own = 1.0, jax.random.fold_in(stream_key, 6)
    for position, blocks in split:
        heights = jnp.exp(jax.random.uniform(jax.random.fold_in(own, position), (blocks,), jnp.float32, least / len(split), high / len(split)))
        factor_of = factor_of * jnp.repeat(heights, extent[position] // blocks).reshape([-1 if axis == position else 1 for axis in range(len(extent))])
    return factor_of


def routed_block(stream_key, own, number, rows, number_of, top, reach, skew):
    ranking = jax.random.permutation(stream_key, number_of)
    crowded, ordinary = load_shares(number_of, rows * top, reach, skew, True), load_shares(number_of, rows * top, reach, skew, False)
    places = jnp.arange(number_of)

    def named(tallies, turn):
        used = int((tallies > 0).sum())
        fixed = max(1, used // 4)
        moved = fixed + (places - fixed + turn * (used - fixed)) % max(1, number_of - fixed)
        return jnp.zeros((number_of,), jnp.int32).at[ranking[jnp.where(places < fixed, places, moved)]].set(jnp.asarray(tallies, jnp.int32))

    tallies = jnp.where(number % 4 == 0, named(crowded, number // 4), named(ordinary, number - number // 4 - 1))
    mixed = jax.random.permutation(jax.random.fold_in(own, 3), number_of)
    giver, taker = mixed[0:number_of // 2 * 2:2], mixed[1:number_of // 2 * 2:2]
    slack = jnp.minimum(tallies[giver] - 1, reach - tallies[taker]) // 2
    slack = jnp.where((giver == ranking[0]) | (taker == ranking[0]) | (tallies[taker] == 0), 0, jnp.maximum(slack, 0))
    moved = jax.random.randint(jax.random.fold_in(own, 4), (number_of // 2,), 0, 1 << 20) % (slack + 1)
    tallies = tallies.at[giver].add(-moved).at[taker].add(moved)
    items = jnp.searchsorted(jnp.cumsum(tallies), jnp.arange(rows * top), side="right").astype(jnp.int32)
    listing = items.reshape(top, rows).T
    listing = listing[jax.random.permutation(jax.random.fold_in(own, 1), rows)]
    turn = jax.random.randint(jax.random.fold_in(own, 2), (rows, 1), 0, top)
    return jnp.take_along_axis(listing, (jnp.arange(top)[None, :] + turn) % top, axis=1)


def load_shares(number_of, total, limit, skew, full):
    loads = [(1 << 20) // math.isqrt(standing ** skew) + 1 for standing in range(1, number_of + 1)]
    largest = limit if full else min(limit, max(-(-total // number_of), total * loads[0] // sum(loads)))
    least = 1 if total - largest >= number_of - 1 else 0
    counts, spare = [largest] + [least] * (number_of - 1), total - largest - least * (number_of - 1)
    while spare > 0:
        movable = [i for i in range(1, number_of) if counts[i] < largest] or [i for i in range(1, number_of) if counts[i] < limit]
        mass, remaining = sum([loads[i] for i in movable]), spare
        for i in movable:
            more = min(limit - counts[i], max(1, remaining * loads[i] // mass), spare)
            counts[i] = counts[i] + more
            spare = spare - more
    return np.array(counts)


def gaussian(own_key, dims, deviation, limit, pieces=(), held_as=jnp.bfloat16):
    drawn = jax.random.normal(own_key, dims, jnp.float32) * deviation
    if len(pieces) > 0:
        drawn = level_of(own_key, dims, pieces, -0.22, 0.18) * drawn
    return jnp.clip(drawn, min=-limit, max=limit).astype(held_as)


def setup_inputs(seed: int = 0) -> dict:
    key_of = jax.random.split(jax.random.key(seed), 8)
    tokens = gaussian(key_of[0], (TOKENS, D), 1.0, 6.0, ((0, 768),))
    routes_keys = jax.random.split(jax.random.fold_in(key_of[1], 1), TOKENS // TOK_DEV)
    routes_turns = jax.random.permutation(jax.random.fold_in(key_of[1], 3), TOKENS // TOK_DEV)
    routes = jax.vmap(lambda own, number: routed_block(jax.random.fold_in(key_of[1], 2), own, number, TOK_DEV, EXPERTS, TOP, CAP, 2))(routes_keys, routes_turns).reshape((TOKENS, TOP))
    route_gates = jnp.clip(jnp.exp(math.log(1.0) - 2.3025851 * jax.random.uniform(key_of[2], (TOKENS, TOP), jnp.float32) ** level_of(key_of[2], (TOKENS, TOP), ((0, 768),), -0.2, 0.2)), 0.1, 1.0)
    w_gate = gaussian(key_of[3], (EXPERTS, D, FF), D ** -0.5, 0.125, ((0, 16),))
    w_up = gaussian(key_of[4], (EXPERTS, D, FF), D ** -0.5, 0.125, ((0, 16),))
    w_down = gaussian(key_of[5], (EXPERTS, FF, D), FF ** -0.5, 0.3125, ((0, 16),))
    cotangent = gaussian(key_of[6], (TOKENS, D), 1.0, 6.0, ((0, 768),))
    return {"tokens": tokens, "routes": routes, "route_gates": route_gates, "w_gate": w_gate, "w_up": w_up, "w_down": w_down, "cotangent": cotangent}


def reference(tokens, routes, route_gates, w_gate, w_up, w_down, cotangent):
    flattened = routes.reshape(-1)
    gate_flat = route_gates.reshape(-1)
    bound_rows = N_DP * N_EXPERT * CAP
    grad_scale = 1.0 / ((TOP * TOK_DEV * N_DP) ** 0.5)

    def per_expert(state_tuple, expert_id):
        mixed_acc, tokens_acc, gates_acc = state_tuple
        is_routed = flattened == expert_id
        row_index = jnp.nonzero(is_routed, size=bound_rows, fill_value=0)[0].astype(jnp.int32)
        is_live = jnp.arange(bound_rows, dtype=jnp.int32) < jnp.sum(is_routed.astype(jnp.int32))
        token_row = (row_index // TOP).astype(jnp.int32)
        expert_input = jnp.where(is_live[:, None], tokens[token_row], jnp.zeros((), tokens.dtype))
        gate_value = jnp.where(is_live, gate_flat[row_index], jnp.zeros((), gate_flat.dtype))
        gate_matrix = w_gate[expert_id]
        up_matrix = w_up[expert_id]
        down_matrix = w_down[expert_id]
        pre_gate = jnp.dot(expert_input, gate_matrix, preferred_element_type=jnp.float32)
        pre_up = jnp.dot(expert_input, up_matrix, preferred_element_type=jnp.float32)
        sigmoid_gate = jax.nn.sigmoid(pre_gate)
        hidden = (pre_gate * sigmoid_gate * pre_up).astype(jnp.bfloat16)
        expert_out = jnp.dot(hidden, down_matrix, preferred_element_type=jnp.float32).astype(jnp.bfloat16)
        out_wide = expert_out.astype(jnp.float32)
        mixed_acc = mixed_acc.at[token_row].add(gate_value[:, None] * out_wide)
        grad_rows = cotangent[token_row].astype(jnp.float32)
        inner_sum = jnp.sum(grad_rows * out_wide, axis=1)
        gates_acc = gates_acc.at[row_index].add(jnp.where(is_live, inner_sum, jnp.zeros((), inner_sum.dtype)))
        grad_out = (gate_value[:, None] * grad_rows).astype(jnp.bfloat16)
        grad_hidden = jnp.dot(grad_out, down_matrix.T, preferred_element_type=jnp.float32)
        grad_gate = (grad_hidden * pre_up * sigmoid_gate * (1.0 + pre_gate * (1.0 - sigmoid_gate))).astype(jnp.bfloat16)
        grad_up = (grad_hidden * pre_gate * sigmoid_gate).astype(jnp.bfloat16)
        grad_input = (jnp.dot(grad_gate, gate_matrix.T, preferred_element_type=jnp.float32)
                      + jnp.dot(grad_up, up_matrix.T, preferred_element_type=jnp.float32)).astype(jnp.bfloat16)
        tokens_acc = tokens_acc.at[token_row].add(grad_input.astype(jnp.float32))
        down_grad = (jnp.dot(hidden.T, grad_out, preferred_element_type=jnp.float32) * grad_scale).astype(jnp.bfloat16)
        return (mixed_acc, tokens_acc, gates_acc), down_grad

    start_state = (jnp.zeros((TOKENS, D), jnp.float32), jnp.zeros((TOKENS, D), jnp.float32),
                   jnp.zeros((TOKENS * TOP,), jnp.float32))
    final_state, down_all = lax.scan(per_expert, start_state, jnp.arange(EXPERTS, dtype=jnp.int32))
    mixed_acc, tokens_acc, gates_acc = final_state
    return (mixed_acc.astype(jnp.bfloat16), tokens_acc.astype(jnp.bfloat16),
            gates_acc.reshape(TOKENS, TOP), down_all)
```

```python
import functools
import math

import jax
import jax.numpy as jnp
from jax import lax
from jax.experimental import pallas as pl
from jax.experimental.pallas import tpu as pltpu
from jax.sharding import Mesh
from jax.sharding import PartitionSpec as P

BF = jnp.bfloat16
F32 = jnp.float32
EXPERT = ("zlo", "x")
VMEM_BYTES = 40 * 1024 * 1024


def dot(a, b, ca=1, cb=0):
    return lax.dot_general(a, b, (((ca,), (cb,)), ((), ())), preferred_element_type=F32)


def picks(base, rows, cap, part):
    q = lax.broadcasted_iota(jnp.int32, (rows, base.shape[1]), 0)
    return jnp.where(q == base + part * cap, 1.0, 0.0).astype(BF)


def column(row):
    n = row.shape[1]
    eye = lax.broadcasted_iota(jnp.int32, (n, n), 0) == lax.broadcasted_iota(jnp.int32, (n, n), 1)
    return jnp.sum(jnp.where(eye, row, jnp.zeros((), row.dtype)), axis=1, keepdims=True)


def dispatch_kernel(experts, cap, routes_ref, gates_ref, tok_ref, cot_ref, send_ref, base_ref):
    rows, width = tok_ref.shape
    half = width // 2
    routes = routes_ref[...]
    named = lax.broadcasted_iota(jnp.int32, (experts, rows), 0) == routes
    before = lax.broadcasted_iota(jnp.int32, (rows, rows), 0) < lax.broadcasted_iota(
        jnp.int32, (rows, rows), 1
    )
    earlier = dot(
        jnp.where(named, 1.0, 0.0).astype(BF), jnp.where(before, 1.0, 0.0).astype(BF)
    )
    slot = jnp.sum(jnp.where(named, earlier, 0.0), axis=0, keepdims=True).astype(jnp.int32)
    base = routes * (4 * cap) + slot
    base_ref[...] = jnp.broadcast_to(base, base_ref.shape)
    graded = (column(gates_ref[...]) * cot_ref[...].astype(F32)).astype(BF)
    tok = tok_ref[...]
    sources = jnp.concatenate(
        [tok[:, :half], tok[:, half:], graded[:, :half], graded[:, half:]], axis=0
    )
    slots = send_ref.shape[0]
    pick = jnp.concatenate([picks(base, slots, cap, part) for part in range(4)], axis=1)
    send_ref[...] = dot(pick, sources).astype(BF)


def expert_kernel(
    ranks, cap, scale, place_ref, got_ref, wg_ref, wu_ref, wd_ref, back_ref, keep_ref, give_ref, prod_ref
):
    slots, half = got_ref.shape
    n = ranks * cap
    r = lax.broadcasted_iota(jnp.int32, (n, slots), 0)
    q = lax.broadcasted_iota(jnp.int32, (n, slots), 1)
    got = got_ref[...]
    source = (r // cap) * (4 * cap) + r % cap
    pick = [jnp.where(q == source + part * cap, 1.0, 0.0).astype(BF) for part in range(4)]
    x0, x1, g0, g1 = (dot(p, got).astype(BF) for p in pick)
    x = jnp.concatenate([x0, x1], axis=1)
    g = jnp.concatenate([g0, g1], axis=1)
    pre_gate = dot(x, wg_ref[...])
    pre_up = dot(x, wu_ref[...])
    s = jax.nn.sigmoid(pre_gate)
    hidden = (pre_gate * s * pre_up).astype(BF)
    prod_ref[...] = dot(hidden, g, 0, 0) * scale
    zhi, y, core = place_ref[0], place_ref[1], place_ref[2]
    ring, line, depth, _ = keep_ref.shape
    for k in range(ring):
        for j in range(line):
            chip = lax.rem(zhi + j, line) * ring + lax.rem(y + k, ring)
            mine = pl.multiple_of((2 * chip + core) * depth, depth)
            theirs = pl.multiple_of((2 * chip + 1 - core) * depth, depth)
            keep_ref[k, j] = prod_ref[pl.ds(mine, depth), :]
            give_ref[k, j] = prod_ref[pl.ds(theirs, depth), :].astype(BF)
    out = dot(hidden, wd_ref[...]).astype(BF)
    grad_hidden = dot(g, wd_ref[...], 1, 1)
    grad_gate = (grad_hidden * pre_up * s * (1.0 + pre_gate * (1.0 - s))).astype(BF)
    grad_up = (grad_hidden * pre_gate * s).astype(BF)
    grad_in = (dot(grad_gate, wg_ref[...], 1, 1) + dot(grad_up, wu_ref[...], 1, 1)).astype(BF)
    packed = dot(pick[0], out[:, :half], 0, 0)
    packed += dot(pick[1], out[:, half:], 0, 0)
    packed += dot(pick[2], grad_in[:, :half], 0, 0)
    packed += dot(pick[3], grad_in[:, half:], 0, 0)
    back_ref[...] = packed.astype(BF)


def collect_kernel(cap, base_ref, gates_ref, cot_ref, back_ref, mixed_ref, dtok_ref, dgate_ref):
    rows, width = cot_ref.shape
    half = width // 2
    slots = back_ref.shape[0]
    base = base_ref[0:1, :]
    back = back_ref[...]
    take = [dot(picks(base, slots, cap, part), back, 0, 0) for part in range(4)]
    gate = column(gates_ref[...])
    mixed_ref[:, :half] = (gate * take[0]).astype(BF)
    mixed_ref[:, half:] = (gate * take[1]).astype(BF)
    dtok_ref[:, :half] = take[2].astype(BF)
    dtok_ref[:, half:] = take[3].astype(BF)
    inner = jnp.sum(cot_ref[:, :half].astype(F32) * take[0], axis=1, keepdims=True)
    inner += jnp.sum(cot_ref[:, half:].astype(F32) * take[1], axis=1, keepdims=True)
    eye = lax.broadcasted_iota(jnp.int32, (rows, rows), 0) == lax.broadcasted_iota(
        jnp.int32, (rows, rows), 1
    )
    dgate_ref[...] = jnp.sum(jnp.where(eye, inner, 0.0), axis=0, keepdims=True)


def onchip(x):
    return pltpu.with_memory_space_constraint(x, pltpu.VMEM)


def tree(parts):
    terms = [part.astype(F32) for part in parts]
    while len(terms) > 1:
        terms = [sum(terms[i : i + 2][1:], terms[i]) for i in range(0, len(terms), 2)]
    return terms[0].astype(BF)


def pair_kernel(keep_ref, other_ref, *pair_refs):
    for k, ref in enumerate(pair_refs):
        ref[...] = (keep_ref[k] + other_ref[k].astype(F32)).astype(BF)


def ring_kernel(*refs):
    line = refs[0].shape[0]
    for j in range(line):
        refs[len(refs) - line + j][...] = tree([ref[j] for ref in refs[: len(refs) - line]])


def whole(count):
    return [pl.BlockSpec(memory_space=pltpu.VMEM)] * count


def per_device(tokens, routes, route_gates, w_gate, w_up, w_down, cotangent):
    rows, width = tokens.shape
    ranks = lax.axis_size(EXPERT)
    experts = w_gate.shape[0] * ranks
    ff = w_gate.shape[2]
    dp = lax.axis_size(("zhi", "y", "core"))
    zhi, ring, cores = (lax.axis_size(a) for a in ("zhi", "y", "core"))
    cap = 5 * rows * routes.shape[1] // (4 * experts)
    half = width // 2
    slots = 4 * cap * experts
    route_row = routes.reshape(1, rows)
    gate_row = route_gates.reshape(1, rows)
    send, base = pl.pallas_call(
        functools.partial(dispatch_kernel, experts, cap),
        out_shape=(
            jax.ShapeDtypeStruct((slots, half), BF),
            jax.ShapeDtypeStruct((8, rows), jnp.int32),
        ),
        in_specs=whole(4),
        out_specs=tuple(whole(2)),
        compiler_params=pltpu.CompilerParams(vmem_limit_bytes=VMEM_BYTES),
        name="dispatch",
    )(route_row, gate_row, tokens, cotangent)
    got = lax.all_to_all(
        send.reshape(experts, 4 * cap, half), EXPERT, split_axis=0, concat_axis=0, tiled=True
    )
    depth = ff // dp
    scale = 1.0 / math.sqrt(routes.shape[1] * rows * dp)
    place = jnp.stack([lax.axis_index(a) for a in ("zhi", "y", "core")]).astype(jnp.int32)
    back, keep, give = pl.pallas_call(
        functools.partial(expert_kernel, ranks, cap, scale),
        out_shape=(
            jax.ShapeDtypeStruct((slots, half), BF),
            jax.ShapeDtypeStruct((ring, zhi, depth, width), F32),
            jax.ShapeDtypeStruct((ring, zhi, depth, width), BF),
        ),
        in_specs=[pl.BlockSpec(memory_space=pltpu.SMEM)] + whole(4),
        out_specs=tuple(whole(3)),
        scratch_shapes=[pltpu.VMEM((ff, width), F32)],
        compiler_params=pltpu.CompilerParams(vmem_limit_bytes=VMEM_BYTES),
        name="expert",
    )(place, onchip(got.reshape(slots, half)), w_gate[0], w_up[0], w_down[0])
    returned = lax.all_to_all(
        back.reshape(experts, 4 * cap, half), EXPERT, split_axis=0, concat_axis=0, tiled=True
    )
    other = lax.ppermute(give, "core", [(i, cores - 1 - i) for i in range(cores)])
    tile = jax.ShapeDtypeStruct((zhi, depth, width), BF)
    pairs = pl.pallas_call(
        pair_kernel,
        out_shape=(tile,) * ring,
        in_specs=whole(2),
        out_specs=tuple(whole(ring)),
        compiler_params=pltpu.CompilerParams(vmem_limit_bytes=VMEM_BYTES),
        name="pair",
    )(keep, onchip(other))
    came = [
        lax.ppermute(pairs[k], "y", [(i, (i + k) % ring) for i in range(ring)])
        for k in range(1, ring)
    ]
    tile = jax.ShapeDtypeStruct((depth, width), BF)
    lines = pl.pallas_call(
        ring_kernel,
        out_shape=(tile,) * zhi,
        in_specs=whole(ring),
        out_specs=tuple(whole(zhi)),
        compiler_params=pltpu.CompilerParams(vmem_limit_bytes=VMEM_BYTES),
        name="ringsum",
    )(pairs[0], *came)
    last = [
        lax.ppermute(lines[j], "zhi", [(i, (i + j) % zhi) for i in range(zhi)])
        for j in range(1, zhi)
    ]
    d_w_down = tree([lines[0], *last])[None]
    mixed, d_tokens, d_gates = pl.pallas_call(
        functools.partial(collect_kernel, cap),
        out_shape=(
            jax.ShapeDtypeStruct((rows, width), BF),
            jax.ShapeDtypeStruct((rows, width), BF),
            jax.ShapeDtypeStruct((1, rows), F32),
        ),
        in_specs=whole(4),
        out_specs=tuple(whole(3)),
        compiler_params=pltpu.CompilerParams(vmem_limit_bytes=VMEM_BYTES),
        name="collect",
    )(base, gate_row, cotangent, onchip(returned.reshape(slots, half)))
    return (mixed, d_tokens, d_gates.reshape(rows, 1), d_w_down)


def physical(mesh):
    dp, expert = (mesh.shape[a] for a in ("dp", "expert"))
    sizes = (3, dp // 6, 2, 4, expert // 4)
    return Mesh(mesh.devices.reshape(sizes), ("zhi", "y", "core", "zlo", "x"))


def solution(mesh):
    dp = ("zhi", "y", "core")
    every = P(dp + EXPERT, None)
    weight = P(EXPERT, None, None)
    return jax.shard_map(
        per_device,
        mesh=physical(mesh),
        in_specs=(every, every, every, weight, weight, weight, every),
        out_specs=(every, every, every, P(EXPERT, dp, None)),
        check_vma=False,
    )
```

```python
import functools
import math

import jax
import jax.numpy as jnp
from jax import lax
from jax.experimental import pallas as pl
from jax.experimental.pallas import tpu as pltpu
from jax.sharding import Mesh
from jax.sharding import PartitionSpec as P

BF = jnp.bfloat16
F32 = jnp.float32
DP = ("zhi", "y", "core")
EXPERT = ("zlo", "x")
EVERY = DP + EXPERT
VMEM_BYTES = 16 * 1024 * 1024
MAIN = 8
PARTS = 4


def dot(a, b, ca=1, cb=0):
    return lax.dot_general(a, b, (((ca,), (cb,)), ((), ())), preferred_element_type=F32)


def iota(shape, axis):
    return lax.broadcasted_iota(jnp.int32, shape, axis)


def where_bf(cond):
    return jnp.where(cond, 1.0, 0.0).astype(BF)


def picks(row, count):
    return where_bf(iota((count, row.shape[1]), 0) == row)


def column(row):
    n = row.shape[1]
    return jnp.sum(
        jnp.where(iota((n, n), 0) == iota((n, n), 1), row, jnp.zeros((), row.dtype)),
        axis=1,
        keepdims=True,
    )


def move(src, dst, sem):
    copy = pltpu.make_async_copy(src, dst, sem)
    copy.start()
    return copy


def dispatch_kernel(
    experts, routes_ref, gates_ref, tok_ref, cot_ref, send_ref, rows_ref, tok, cot, made, sem
):
    tokens, width = tok.shape
    half = width // 2
    first = move(tok_ref, tok, sem.at[0])
    second = move(cot_ref, cot, sem.at[1])
    routes = routes_ref[...]
    named = iota((experts, tokens), 0) == routes
    earlier = dot(
        where_bf(named), where_bf(iota((tokens, tokens), 0) < iota((tokens, tokens), 1))
    )
    slot = jnp.sum(jnp.where(named, earlier, 0.0), axis=0, keepdims=True).astype(jnp.int32)
    straight = jnp.where(slot < MAIN, routes * MAIN + slot, -1)
    folded = jnp.where(slot < MAIN, -PARTS, routes * MAIN + (slot - MAIN) * PARTS)
    rows_ref[...] = jnp.where(iota(rows_ref.shape, 0) == 0, straight, folded)
    gate = column(gates_ref[...])
    slots = send_ref.shape[0]
    pick = picks(straight, slots)
    fold = jnp.concatenate([picks(folded + part, slots) for part in range(PARTS)], axis=1)
    spans = [pl.ds(0, width), pl.ds(width, width), pl.ds(2 * width, half)]
    first.wait()
    plain = tok[...]
    made[:, :width] = dot(pick, plain).astype(BF)
    out = [move(made.at[:, spans[0]], send_ref.at[:, spans[0]], sem.at[2])]
    second.wait()
    graded = (gate * cot[...].astype(F32)).astype(BF)
    made[:, width : 2 * width] = dot(pick, graded).astype(BF)
    out.append(move(made.at[:, spans[1]], send_ref.at[:, spans[1]], sem.at[3]))
    sources = jnp.concatenate(
        [plain[:, :half], plain[:, half:], graded[:, :half], graded[:, half:]], axis=0
    )
    made[:, 2 * width :] = dot(fold, sources).astype(BF)
    out.append(move(made.at[:, spans[2]], send_ref.at[:, spans[2]], sem.at[4]))
    for copy in out:
        copy.wait()


def unfold(ranks, spare, part):
    shape = (ranks * spare, ranks * MAIN)
    r, q = iota(shape, 0), iota(shape, 1)
    return where_bf(q == (r // spare) * MAIN + (r % spare) * PARTS + part)


def product(hidden, grads, place_ref, blocks, own, scale):
    zhi, y, core = place_ref[0], place_ref[1], place_ref[2]
    sides, steps, line, depth, _ = blocks
    ring = sides * steps
    shape = (hidden.shape[1], sides * steps * line * depth)
    want = iota(shape, 1)
    side, rest = want // (steps * line * depth), want % (steps * line * depth)
    m, rest = rest // (line * depth), rest % (line * depth)
    j, row = rest // depth, rest % depth
    at = jnp.where(side == 0, y, lax.bitwise_xor(y, 1)) + 2 * m
    at = jnp.where(at >= ring, at - ring, at)
    up = zhi + j
    up = jnp.where(up >= line, up - line, up)
    chosen = core if own else 1 - core
    source = ((up * ring + at) * 2 + chosen) * depth + row
    ordered = dot(hidden, where_bf(iota(shape, 0) == source)).astype(BF)
    return (dot(ordered, grads, 0, 0) * scale).reshape(blocks)


def forward_kernel(
    ranks, spare, scale, place_ref, got_ref, wg_ref, wu_ref, give_ref, grad_ref, gate_ref, up_ref
):
    width = grad_ref.shape[1]
    fold = got_ref[:, 2 * width :]
    extra = [dot(unfold(ranks, spare, part), fold).astype(BF) for part in range(PARTS)]
    x = jnp.concatenate(
        [got_ref[:, :width], jnp.concatenate([extra[0], extra[1]], axis=1)], axis=0
    )
    g = jnp.concatenate(
        [got_ref[:, width : 2 * width], jnp.concatenate([extra[2], extra[3]], axis=1)], axis=0
    )
    grad_ref[...] = g
    pre_gate = dot(x, wg_ref[...])
    gate_ref[...] = pre_gate
    pre_up = dot(x, wu_ref[...])
    up_ref[...] = pre_up
    hidden = (pre_gate * jax.nn.sigmoid(pre_gate) * pre_up).astype(BF)
    give_ref[...] = product(hidden, g, place_ref, give_ref.shape, False, scale).astype(BF)


def backward_kernel(
    ranks, spare, scale, place_ref, grad_ref, gate_ref, up_ref, wd_ref, wg_ref, wu_ref,
    back_ref, keep_ref, made, wg, wu, sem,
):
    width = grad_ref.shape[1]
    half = width // 2
    straight = ranks * MAIN
    spans = [pl.ds(0, width), pl.ds(width, width), pl.ds(2 * width, half)]
    loads = [move(wg_ref, wg, sem.at[0]), move(wu_ref, wu, sem.at[1])]
    pre_gate, pre_up = gate_ref[...], up_ref[...]
    s = jax.nn.sigmoid(pre_gate)
    hidden = (pre_gate * s * pre_up).astype(BF)
    out = dot(hidden, wd_ref[...]).astype(BF)
    made[:, :width] = out[:straight]
    sent = [move(made.at[:, spans[0]], back_ref.at[:, spans[0]], sem.at[2])]
    grads = grad_ref[...]
    grad_hidden = dot(grads, wd_ref[...], 1, 1)
    grad_gate = (grad_hidden * pre_up * s * (1.0 + pre_gate * (1.0 - s))).astype(BF)
    grad_up = (grad_hidden * pre_gate * s).astype(BF)
    for load in loads:
        load.wait()
    grad_in = (dot(grad_gate, wg[...], 1, 1) + dot(grad_up, wu[...], 1, 1)).astype(BF)
    made[:, width : 2 * width] = grad_in[:straight]
    sent.append(move(made.at[:, spans[1]], back_ref.at[:, spans[1]], sem.at[3]))
    pieces = [out[straight:, :half], out[straight:, half:]]
    pieces += [grad_in[straight:, :half], grad_in[straight:, half:]]
    fold = [dot(unfold(ranks, spare, part), piece, 0, 0) for part, piece in enumerate(pieces)]
    made[:, 2 * width :] = (fold[0] + fold[1] + fold[2] + fold[3]).astype(BF)
    sent.append(move(made.at[:, spans[2]], back_ref.at[:, spans[2]], sem.at[4]))
    keep_ref[...] = product(hidden, grads, place_ref, keep_ref.shape, True, scale)
    for copy in sent:
        copy.wait()


def collect_kernel(rows_ref, gates_ref, cot_ref, back_ref, mixed_ref, dtok_ref, dgate_ref):
    tokens, width = cot_ref.shape
    half = width // 2
    slots = back_ref.shape[0]
    pick = picks(rows_ref[0:1, :], slots)
    folded = rows_ref[1:2, :]
    gate = column(gates_ref[...])
    inner = jnp.zeros((tokens, 1), F32)
    for part in range(PARTS):
        lanes = slice(part * half, (part + 1) * half)
        taken = dot(pick, back_ref[:, lanes], 0, 0)
        taken += dot(picks(folded + part, slots), back_ref[:, 2 * width :], 0, 0)
        if part < 2:
            mixed_ref[:, lanes] = (gate * taken).astype(BF)
            inner += jnp.sum(cot_ref[:, lanes].astype(F32) * taken, axis=1, keepdims=True)
        else:
            dtok_ref[:, part * half - width : (part + 1) * half - width] = taken.astype(BF)
    same = iota((tokens, tokens), 0) == iota((tokens, tokens), 1)
    dgate_ref[...] = jnp.sum(jnp.where(same, inner, 0.0), axis=0, keepdims=True)


def tree(parts):
    terms = [part.astype(F32) for part in parts]
    while len(terms) > 1:
        terms = [sum(terms[i : i + 2][1:], terms[i]) for i in range(0, len(terms), 2)]
    return terms[0]


def core_sum_kernel(keep_ref, other_ref, own_ref, give_ref):
    own_ref[...] = keep_ref[0] + other_ref[0].astype(F32)
    give_ref[...] = (keep_ref[1] + other_ref[1].astype(F32)).astype(BF)


def side_sum_kernel(own_ref, came_ref, *refs):
    for m, ref in enumerate(refs):
        ref[...] = (own_ref[m] + came_ref[m].astype(F32)).astype(ref.dtype)


def ring_sum_kernel(*refs):
    line = refs[0].shape[0]
    terms, sums = refs[: len(refs) - line], refs[len(refs) - line :]
    for j, ref in enumerate(sums):
        ref[...] = tree([term[j] for term in terms]).astype(ref.dtype)


def vmem(count):
    return [pl.BlockSpec(memory_space=pltpu.VMEM)] * count


def local(kernel, inputs, outputs, in_specs=None, out_specs=None, flops=0, **extra):
    return pl.pallas_call(
        kernel,
        out_shape=tuple(outputs),
        in_specs=in_specs or vmem(len(inputs)),
        out_specs=tuple(out_specs or vmem(len(outputs))),
        compiler_params=pltpu.CompilerParams(vmem_limit_bytes=VMEM_BYTES),
        cost_estimate=pl.CostEstimate(flops=flops, bytes_accessed=1 << 20, transcendentals=0),
        **extra,
    )(*inputs)


def onchip(x):
    return pltpu.with_memory_space_constraint(x, pltpu.VMEM)


def shaped(shape, dtype):
    return jax.ShapeDtypeStruct(shape, dtype)


def exchange_groups(zhi, ring, cores, zlo, xs):
    groups = []
    for core in range(cores):
        for window in range(zhi):
            for y in range(ring):
                group = []
                for z in range(zlo):
                    at = window if core == 0 or z >= zlo // 2 else (window + 1) % zhi
                    group += [(((at * ring + y) * cores + core) * zlo + z) * xs + x for x in range(xs)]
                groups.append(group)
    return groups


def per_device(tokens, routes, route_gates, w_gate, w_up, w_down, cotangent):
    rows, width = tokens.shape
    ranks = lax.axis_size(EXPERT)
    ff = w_gate.shape[2]
    zhi, ring, cores = (lax.axis_size(a) for a in DP)
    dp = zhi * ring * cores
    cap = 5 * rows * routes.shape[1] // (4 * ranks)
    spare = cap - MAIN
    lanes = 2 * width + width // 2
    groups = exchange_groups(zhi, ring, cores, *(lax.axis_size(a) for a in EXPERT))

    def exchange(values):
        return lax.all_to_all(
            values.reshape(ranks, MAIN, lanes),
            EVERY,
            split_axis=0,
            concat_axis=0,
            axis_index_groups=groups,
            tiled=True,
        ).reshape(ranks * MAIN, lanes)

    route_row = routes.reshape(1, rows)
    gate_row = route_gates.reshape(1, rows)
    far_off = pl.BlockSpec(memory_space=pltpu.HBM)
    anywhere = pl.BlockSpec(memory_space=pl.ANY)
    scalars = pl.BlockSpec(memory_space=pltpu.SMEM)
    slots = ranks * MAIN
    send, base = pl.pallas_call(
        functools.partial(dispatch_kernel, ranks),
        out_shape=(pltpu.HBM((slots, lanes), BF), shaped((8, rows), jnp.int32)),
        in_specs=vmem(2) + [anywhere] * 2,
        out_specs=(far_off, vmem(1)[0]),
        scratch_shapes=[
            pltpu.VMEM((rows, width), BF),
            pltpu.VMEM((rows, width), BF),
            pltpu.VMEM((slots, lanes), BF),
            pltpu.SemaphoreType.DMA((5,)),
        ],
        name="dispatch",
    )(route_row, gate_row, tokens, cotangent)
    got = exchange(send)
    depth = ff // dp
    scale = 1.0 / math.sqrt(routes.shape[1] * rows * dp)
    place = jnp.stack([lax.axis_index(a) for a in DP]).astype(jnp.int32)
    blocks = (2, ring // 2, zhi, depth, width)
    staged = [pltpu.VMEM((width, ff), BF), pltpu.VMEM((width, ff), BF)]
    give, grads, pre_gate, pre_up = local(
        functools.partial(forward_kernel, ranks, spare, scale),
        (place, onchip(got), w_gate[0], w_up[0]),
        [
            pltpu.VMEM(blocks, BF),
            pltpu.VMEM((ranks * cap, width), BF),
            pltpu.VMEM((ranks * cap, ff), F32),
            pltpu.VMEM((ranks * cap, ff), F32),
        ],
        in_specs=[scalars] + vmem(3),
        flops=6 * ranks * cap * ff * width,
    )
    other = lax.ppermute(give, "core", [(i, cores - 1 - i) for i in range(cores)])
    back, keep = local(
        functools.partial(backward_kernel, ranks, spare, scale),
        (place, grads, pre_gate, pre_up, w_down[0], w_gate[0], w_up[0]),
        [pltpu.HBM((slots, lanes), BF), pltpu.VMEM(blocks, F32)],
        in_specs=[scalars] + vmem(4) + [anywhere] * 2,
        out_specs=[far_off, vmem(1)[0]],
        flops=10 * ranks * cap * ff * width,
        scratch_shapes=[pltpu.VMEM((slots, lanes), BF)] + staged + [pltpu.SemaphoreType.DMA((5,))],
    )
    returned = exchange(back)
    own, side = local(
        core_sum_kernel,
        (keep, onchip(other)),
        [pltpu.VMEM(blocks[1:], F32), pltpu.VMEM(blocks[1:], BF)],
    )
    came = lax.ppermute(side, "y", [(i, i ^ 1) for i in range(ring)])
    steps = local(
        side_sum_kernel,
        (own, onchip(came)),
        [pltpu.VMEM(blocks[2:], BF if m else F32) for m in range(ring // 2)],
    )
    far = [
        lax.ppermute(steps[m], "y", [(i, (i + 2 * m) % ring) for i in range(ring)])
        for m in range(1, ring // 2)
    ]
    lines = local(
        ring_sum_kernel,
        (steps[0], *[onchip(f) for f in far]),
        [pltpu.VMEM(blocks[3:], BF if j else F32) for j in range(zhi)],
    )
    last = [
        lax.ppermute(lines[j], "zhi", [(i, (i + j) % zhi) for i in range(zhi)])
        for j in range(1, zhi)
    ]
    d_w_down = tree([lines[0], *last]).astype(BF)[None]
    mixed, d_tokens, d_gates = local(
        collect_kernel,
        (base, gate_row, cotangent, onchip(returned)),
        [shaped((rows, width), BF), shaped((rows, width), BF), shaped((1, rows), F32)],
    )
    return (mixed, d_tokens, d_gates.reshape(rows, 1), d_w_down)


def physical(mesh):
    dp, expert = (mesh.shape[a] for a in ("dp", "expert"))
    return Mesh(mesh.devices.reshape(3, dp // 6, 2, 4, expert // 4), EVERY)


def solution(mesh):
    every = P(EVERY, None)
    weight = P(EXPERT, None, None)
    return jax.shard_map(
        per_device,
        mesh=physical(mesh),
        in_specs=(every, every, every, weight, weight, weight, every),
        out_specs=(every, every, every, P(EXPERT, DP, None)),
        check_vma=False,
    )
```

```python
import functools
import math

import jax
import jax.numpy as jnp
from jax import lax
from jax.experimental import pallas as pl
from jax.experimental.pallas import tpu as pltpu
from jax.sharding import Mesh
from jax.sharding import PartitionSpec as P

BF = jnp.bfloat16
F32 = jnp.float32
DP = ("zhi", "y", "core")
EXPERT = ("zlo", "x")
EVERY = DP + EXPERT
VMEM_BYTES = 24 * 1024 * 1024
MAIN = 8
PARTS = 4


def dot(a, b, ca=1, cb=0):
    return lax.dot_general(a, b, (((ca,), (cb,)), ((), ())), preferred_element_type=F32)


def iota(shape, axis):
    return lax.broadcasted_iota(jnp.int32, shape, axis)


def where_bf(cond):
    return jnp.where(cond, 1.0, 0.0).astype(BF)


def picks(row, count):
    return where_bf(iota((count, row.shape[1]), 0) == row)


def column(row):
    n = row.shape[1]
    return jnp.sum(
        jnp.where(iota((n, n), 0) == iota((n, n), 1), row, jnp.zeros((), row.dtype)),
        axis=1,
        keepdims=True,
    )


def move(src, dst, sem):
    copy = pltpu.make_async_copy(src, dst, sem)
    copy.start()
    return copy


def dispatch_kernel(
    experts, routes_ref, gates_ref, tok_ref, cot_ref, send_ref, rows_ref, held, made, sem
):
    _, tokens, half = held.shape
    loads = []
    for part in range(PARTS):
        lanes = pl.ds((part % 2) * half, half)
        source = tok_ref if part < 2 else cot_ref
        loads.append(move(source.at[:, lanes], held.at[part], sem.at[part]))
    routes = routes_ref[...]
    named = iota((experts, tokens), 0) == routes
    earlier = dot(
        where_bf(named), where_bf(iota((tokens, tokens), 0) < iota((tokens, tokens), 1))
    )
    slot = jnp.sum(jnp.where(named, earlier, 0.0), axis=0, keepdims=True).astype(jnp.int32)
    straight = jnp.where(slot < MAIN, routes * MAIN + slot, -1)
    folded = jnp.where(slot < MAIN, -PARTS, routes * MAIN + (slot - MAIN) * PARTS)
    rows_ref[...] = jnp.where(iota(rows_ref.shape, 0) == 0, straight, folded)
    gate = column(gates_ref[...])
    slots = send_ref.shape[0]
    pick = picks(straight, slots)
    stores = []

    def store(part):
        lanes = pl.ds(part * half, half)
        stores.append(move(made.at[:, lanes], send_ref.at[:, lanes], sem.at[PARTS + part]))

    fold = jnp.zeros((slots, half), F32)
    for part in range(PARTS):
        loads[part].wait()
        value = held[part]
        if part >= 2:
            value = (gate * value.astype(F32)).astype(BF)
        made[:, part * half : (part + 1) * half] = dot(pick, value).astype(BF)
        store(part)
        fold += dot(picks(folded + part, slots), value)
    made[:, PARTS * half :] = fold.astype(BF)
    store(PARTS)
    for copy in stores:
        copy.wait()


def unfold(ranks, spare, part):
    shape = (ranks * spare, ranks * MAIN)
    r, q = iota(shape, 0), iota(shape, 1)
    return where_bf(q == (r // spare) * MAIN + (r % spare) * PARTS + part)


def product(hidden, grads, place_ref, shape, sides, own, scale):
    zhi, y, core = place_ref[0], place_ref[1], place_ref[2]
    steps, line, depth, _ = shape[-4:]
    ring = 2 * steps
    spread = (hidden.shape[1], len(sides) * steps * line * depth)
    want = iota(spread, 1)
    side, rest = want // (steps * line * depth) + sides[0], want % (steps * line * depth)
    m, rest = rest // (line * depth), rest % (line * depth)
    j, row = rest // depth, rest % depth
    at = jnp.where(side == 0, y, lax.bitwise_xor(y, 1)) + 2 * m
    at = jnp.where(at >= ring, at - ring, at)
    up = zhi + j
    up = jnp.where(up >= line, up - line, up)
    chosen = core if own else 1 - core
    source = ((up * ring + at) * 2 + chosen) * depth + row
    ordered = dot(hidden, where_bf(iota(spread, 0) == source)).astype(BF)
    return (dot(ordered, grads, 0, 0) * scale).reshape(shape)


def forward_kernel(
    ranks, spare, scale, place_ref, got_ref, wg_ref, wu_ref, give_ref, grad_ref, hidden_ref,
    gate_ref, up_ref, held, sem,
):
    width = grad_ref.shape[1]
    straight = ranks * MAIN
    spans = [pl.ds(2 * width, width // 2), pl.ds(0, width), pl.ds(width, width)]
    loads = [move(got_ref.at[:, at], held.at[:, at], sem.at[i]) for i, at in enumerate(spans)]
    pick = [unfold(ranks, spare, part) for part in range(PARTS)]
    loads[0].wait()
    fold = held[:, 2 * width :]
    extra = [dot(pick[part], fold).astype(BF) for part in range(PARTS)]
    grad_ref[straight:, :] = jnp.concatenate(extra[2:], axis=1)
    loads[1].wait()
    x = jnp.concatenate([held[:, :width], jnp.concatenate(extra[:2], axis=1)], axis=0)
    pre_gate = dot(x, wg_ref[...])
    gate_ref[...] = pre_gate
    pre_up = dot(x, wu_ref[...])
    up_ref[...] = pre_up
    hidden = (pre_gate * jax.nn.sigmoid(pre_gate) * pre_up).astype(BF)
    hidden_ref[...] = hidden
    loads[2].wait()
    grad_ref[:straight, :] = held[:, width : 2 * width]
    give_ref[...] = product(
        hidden, grad_ref[...], place_ref, give_ref.shape, (0, 1), False, scale
    ).astype(BF)


def core_sum_kernel(scale, place_ref, grad_ref, hidden_ref, other_ref, side_ref):
    made = product(hidden_ref[...], grad_ref[...], place_ref, side_ref.shape, (1,), True, scale)
    side_ref[...] = (made + other_ref[1].astype(F32)).astype(BF)


def backward_kernel(
    ranks, spare, scale, place_ref, grad_ref, hidden_ref, gate_ref, up_ref, wd_ref, wg_ref, wu_ref,
    other_ref, back_ref, own_ref, made, kept, wd, wg, wu, sem,
):
    width = grad_ref.shape[1]
    half = width // 2
    straight = ranks * MAIN
    spans = [pl.ds(0, width), pl.ds(width, width), pl.ds(2 * width, half)]
    first = move(wd_ref, wd, sem.at[5])
    loads = [move(wg_ref, wg, sem.at[0]), move(wu_ref, wu, sem.at[1])]
    hidden, grads = hidden_ref[...], grad_ref[...]
    mine = product(hidden, grads, place_ref, own_ref.shape, (0,), True, scale)
    kept[...] = mine + other_ref[0].astype(F32)
    sent = [move(kept, own_ref, sem.at[6])]
    pre_gate, pre_up = gate_ref[...], up_ref[...]
    s = jax.nn.sigmoid(pre_gate)
    first.wait()
    out = dot(hidden, wd[...]).astype(BF)
    made[:, :width] = out[:straight]
    sent.append(move(made.at[:, spans[0]], back_ref.at[:, spans[0]], sem.at[2]))
    grad_hidden = dot(grads, wd[...], 1, 1)
    grad_gate = (grad_hidden * pre_up * s * (1.0 + pre_gate * (1.0 - s))).astype(BF)
    grad_up = (grad_hidden * pre_gate * s).astype(BF)
    for load in loads:
        load.wait()
    grad_in = (dot(grad_gate, wg[...], 1, 1) + dot(grad_up, wu[...], 1, 1)).astype(BF)
    made[:, width : 2 * width] = grad_in[:straight]
    sent.append(move(made.at[:, spans[1]], back_ref.at[:, spans[1]], sem.at[3]))
    pieces = [out[straight:, :half], out[straight:, half:]]
    pieces += [grad_in[straight:, :half], grad_in[straight:, half:]]
    fold = [dot(unfold(ranks, spare, part), piece, 0, 0) for part, piece in enumerate(pieces)]
    made[:, 2 * width :] = (fold[0] + fold[1] + fold[2] + fold[3]).astype(BF)
    sent.append(move(made.at[:, spans[2]], back_ref.at[:, spans[2]], sem.at[4]))
    for copy in sent:
        copy.wait()


def collect_kernel(rows_ref, gates_ref, cot_ref, back_ref, mixed_ref, dtok_ref, dgate_ref):
    tokens, width = cot_ref.shape
    half = width // 2
    slots = back_ref.shape[0]
    pick = picks(rows_ref[0:1, :], slots)
    folded = rows_ref[1:2, :]
    gate = column(gates_ref[...])
    inner = jnp.zeros((tokens, 1), F32)
    for part in range(PARTS):
        lanes = slice(part * half, (part + 1) * half)
        taken = dot(pick, back_ref[:, lanes], 0, 0)
        taken += dot(picks(folded + part, slots), back_ref[:, 2 * width :], 0, 0)
        if part < 2:
            mixed_ref[:, lanes] = (gate * taken).astype(BF)
            inner += jnp.sum(cot_ref[:, lanes].astype(F32) * taken, axis=1, keepdims=True)
        else:
            dtok_ref[:, part * half - width : (part + 1) * half - width] = taken.astype(BF)
    same = iota((tokens, tokens), 0) == iota((tokens, tokens), 1)
    dgate_ref[...] = jnp.sum(jnp.where(same, inner, 0.0), axis=0, keepdims=True)


def tree(parts):
    terms = [part.astype(F32) for part in parts]
    while len(terms) > 1:
        terms = [sum(terms[i : i + 2][1:], terms[i]) for i in range(0, len(terms), 2)]
    return terms[0]


def side_sum_kernel(own_ref, came_ref, *refs):
    for m, ref in enumerate(refs):
        ref[...] = (own_ref[m] + came_ref[m].astype(F32)).astype(ref.dtype)


def ring_sum_kernel(*refs):
    line = refs[0].shape[0]
    terms, sums = refs[: len(refs) - line], refs[len(refs) - line :]
    for j, ref in enumerate(sums):
        ref[...] = tree([term[j] for term in terms]).astype(ref.dtype)


def vmem(count):
    return [pl.BlockSpec(memory_space=pltpu.VMEM)] * count


def local(kernel, inputs, outputs, in_specs=None, out_specs=None, flops=0, **extra):
    return pl.pallas_call(
        kernel,
        out_shape=tuple(outputs),
        in_specs=in_specs or vmem(len(inputs)),
        out_specs=tuple(out_specs or vmem(len(outputs))),
        compiler_params=pltpu.CompilerParams(vmem_limit_bytes=VMEM_BYTES),
        cost_estimate=pl.CostEstimate(flops=flops, bytes_accessed=1 << 20, transcendentals=0),
        **extra,
    )(*inputs)


def onchip(x):
    return pltpu.with_memory_space_constraint(x, pltpu.VMEM)


def offchip(x):
    return pltpu.with_memory_space_constraint(x, pltpu.HBM)


def shaped(shape, dtype):
    return jax.ShapeDtypeStruct(shape, dtype)


def exchange_groups(zhi, ring, cores, zlo, xs):
    groups = []
    for core in range(cores):
        for window in range(zhi):
            for y in range(ring):
                group = []
                for z in range(zlo):
                    at = window if core == 0 or z >= zlo // 2 else (window + 1) % zhi
                    group += [(((at * ring + y) * cores + core) * zlo + z) * xs + x for x in range(xs)]
                groups.append(group)
    return groups


def per_device(tokens, routes, route_gates, w_gate, w_up, w_down, cotangent):
    rows, width = tokens.shape
    ranks = lax.axis_size(EXPERT)
    ff = w_gate.shape[2]
    zhi, ring, cores = (lax.axis_size(a) for a in DP)
    dp = zhi * ring * cores
    cap = 5 * rows * routes.shape[1] // (4 * ranks)
    spare = cap - MAIN
    lanes = 2 * width + width // 2
    groups = exchange_groups(zhi, ring, cores, *(lax.axis_size(a) for a in EXPERT))

    def exchange(values):
        return lax.all_to_all(
            values.reshape(ranks, MAIN, lanes),
            EVERY,
            split_axis=0,
            concat_axis=0,
            axis_index_groups=groups,
            tiled=True,
        ).reshape(ranks * MAIN, lanes)

    route_row = routes.reshape(1, rows)
    gate_row = route_gates.reshape(1, rows)
    far_off = pl.BlockSpec(memory_space=pltpu.HBM)
    anywhere = pl.BlockSpec(memory_space=pl.ANY)
    scalars = pl.BlockSpec(memory_space=pltpu.SMEM)
    slots = ranks * MAIN
    send, base = pl.pallas_call(
        functools.partial(dispatch_kernel, ranks),
        out_shape=(pltpu.HBM((slots, lanes), BF), shaped((8, rows), jnp.int32)),
        in_specs=vmem(2) + [anywhere] * 2,
        out_specs=(far_off, vmem(1)[0]),
        scratch_shapes=[
            pltpu.VMEM((PARTS, rows, width // 2), BF),
            pltpu.VMEM((slots, lanes), BF),
            pltpu.SemaphoreType.DMA((2 * PARTS + 1,)),
        ],
        name="dispatch",
    )(route_row, gate_row, tokens, cotangent)
    got = exchange(send)
    depth = ff // dp
    scale = 1.0 / math.sqrt(routes.shape[1] * rows * dp)
    place = jnp.stack([lax.axis_index(a) for a in DP]).astype(jnp.int32)
    blocks = (2, ring // 2, zhi, depth, width)
    give, grads, hidden, pre_gate, pre_up = local(
        functools.partial(forward_kernel, ranks, spare, scale),
        (place, got, w_gate[0], w_up[0]),
        [
            pltpu.VMEM(blocks, BF),
            pltpu.VMEM((ranks * cap, width), BF),
            pltpu.VMEM((ranks * cap, ff), BF),
            pltpu.VMEM((ranks * cap, ff), F32),
            pltpu.VMEM((ranks * cap, ff), F32),
        ],
        in_specs=[scalars, anywhere] + vmem(2),
        flops=6 * ranks * cap * ff * width,
        scratch_shapes=[pltpu.VMEM((slots, lanes), BF), pltpu.SemaphoreType.DMA((3,))],
    )
    other = lax.ppermute(give, "core", [(i, cores - 1 - i) for i in range(cores)])
    (side,) = local(
        functools.partial(core_sum_kernel, scale),
        (place, grads, hidden, onchip(other)),
        [pltpu.VMEM(blocks[1:], BF)],
        in_specs=[scalars] + vmem(3),
    )
    back, own = local(
        functools.partial(backward_kernel, ranks, spare, scale),
        (place, grads, hidden, pre_gate, pre_up, *[offchip(w[0]) for w in (w_down, w_gate, w_up)], onchip(other)),
        [pltpu.HBM((slots, lanes), BF), pltpu.HBM(blocks[1:], F32)],
        in_specs=[scalars] + vmem(4) + [anywhere] * 3 + vmem(1),
        out_specs=[far_off] * 2,
        flops=10 * ranks * cap * ff * width,
        scratch_shapes=[
            pltpu.VMEM((slots, lanes), BF),
            pltpu.VMEM(blocks[1:], F32),
            *[pltpu.VMEM(w.shape[1:], BF) for w in (w_down, w_gate, w_up)],
            pltpu.SemaphoreType.DMA((7,)),
        ],
    )
    returned = exchange(back)
    came = lax.ppermute(side, "y", [(i, i ^ 1) for i in range(ring)])
    steps = local(
        side_sum_kernel,
        (own, onchip(came)),
        [pltpu.VMEM(blocks[2:], BF if m else F32) for m in range(ring // 2)],
    )
    far = [
        lax.ppermute(steps[m], "y", [(i, (i + 2 * m) % ring) for i in range(ring)])
        for m in range(1, ring // 2)
    ]
    lines = local(
        ring_sum_kernel,
        (steps[0], *[onchip(f) for f in far]),
        [pltpu.VMEM(blocks[3:], BF if j else F32) for j in range(zhi)],
    )
    last = [
        lax.ppermute(lines[j], "zhi", [(i, (i + j) % zhi) for i in range(zhi)])
        for j in range(1, zhi)
    ]
    d_w_down = tree([lines[0], *last]).astype(BF)[None]
    mixed, d_tokens, d_gates = local(
        collect_kernel,
        (base, gate_row, cotangent, onchip(returned)),
        [shaped((rows, width), BF), shaped((rows, width), BF), shaped((1, rows), F32)],
    )
    return (mixed, d_tokens, d_gates.reshape(rows, 1), d_w_down)


def physical(mesh):
    dp, expert = (mesh.shape[a] for a in ("dp", "expert"))
    return Mesh(mesh.devices.reshape(3, dp // 6, 2, 4, expert // 4), EVERY)


def solution(mesh):
    every = P(EVERY, None)
    weight = P(EXPERT, None, None)
    return jax.shard_map(
        per_device,
        mesh=physical(mesh),
        in_specs=(every, every, every, weight, weight, weight, every),
        out_specs=(every, every, every, P(EXPERT, DP, None)),
        check_vma=False,
    )
```
